128 devices in a mesh: mem: 8 (over z, core), grid: 16 (over x, y).
Axes of the slice: x: 4, y: 4, z: 4, core: 2. Of those that a mesh axis runs over, the one named last changes fastest.
Arguments:
- state: float32 [80, 524288], P('mem', 'grid'), may hold values from -6 to 6
- obs_tile: int32 [4], replicated, may hold values from 0 to 4095
- obs_offset: int32 [4, 256], replicated, may hold values from 0 to 127
- obs_value: float32 [4, 256], replicated, may hold values from -8 to 8
- obs_error: float32 [4, 256], replicated, may hold values from 0.5 to 4
- loc_mask: int32 [4, 4096], replicated, may hold values 0 or 1
- block_order: int32 [4], replicated, may hold values from 0 to 3, each once
Outputs:
- posterior: float32 [80, 524288], P('mem', 'grid')
The draws below stay inside these ranges and needn't reach their ends.
Inputs may be any that keep to these rules, and one draw needn't show every extreme that they name: `block_order`: a permutation of 0 to 3.
All inputs are finite; a program needn't handle non-finite values.
Results may differ from the reference program's by a relative error of at most 0.00024.
Values sent between devices are 32-bit elements; how exact they have to be, the bound alone decides.
A program may use at most 64 MiB of HBM per device.

```python
import math
import jax
import jax.numpy as jnp
from jax import lax

MEMBERS = 80
OBS = 256
BLOCKS = 4
TILE = 128
VALUES = 524288
NTILES = 4096


def set_ends(values, stream_key, smallest, high):
    longest = values.shape.index(max(values.shape))
    spots = []
    for shift in (0, 1):
        where = [jax.random.randint(jax.random.fold_in(stream_key, axis), (), 0, length) for axis, length in enumerate(values.shape)]
        where[longest] = (where[longest] + shift) % values.shape[longest]
        spots.append(tuple(where))
    return values.at[spots[0]].set(smallest).at[spots[1]].set(high)


def block_levels(own_key, dims, shards, low, high):
    def one(axis_at, shards_of):
        steps = jax.random.uniform(jax.random.fold_in(jax.random.fold_in(own_key, 6), axis_at), (shards_of,), jnp.float32, low / len(shards), high / len(shards))
        return jnp.repeat(jnp.exp(steps), dims[axis_at] // shards_of).reshape((-1,) + (1,) * (len(dims) - axis_at - 1))

    gain = one(*shards[0])
    for cut in shards[1:]:
        gain = gain * one(*cut)
    return gain


def scatter_about(key, dims, deviation, reach, cuts=(), held_as=jnp.bfloat16):
    drawn = jax.random.normal(key, dims, jnp.float32) * deviation
    if len(cuts) > 0:
        drawn = block_levels(key, dims, cuts, -0.22, 0.18) * drawn
    return jnp.clip(drawn, min=-reach, max=reach).astype(held_as)


def setup_inputs(seed: int = 0) -> dict:
    key_of = jax.random.split(jax.random.key(seed), 8)
    return {
        "state": scatter_about(key_of[0], (MEMBERS, VALUES), 1.0, 6.0, ((0, 8), (1, 16)), jnp.float32),
        "obs_tile": set_ends(jax.random.randint(key_of[1], (BLOCKS,), 0, NTILES), jax.random.fold_in(key_of[1], 1), 0, NTILES - 1).astype(jnp.int32),
        "obs_offset": set_ends(jax.random.randint(key_of[2], (BLOCKS, OBS), 0, TILE), jax.random.fold_in(key_of[2], 1), 0, TILE - 1).astype(jnp.int32),
        "obs_value": scatter_about(key_of[3], (BLOCKS, OBS), 1.5, 8.0, (), jnp.float32),
        "obs_error": jnp.clip(jnp.exp(jax.random.uniform(key_of[4], (BLOCKS, OBS), jnp.float32, math.log(0.5), math.log(4.0))), 0.5, 4.0),
        "loc_mask": set_ends((jax.random.randint(key_of[5], (BLOCKS, NTILES), 0, 2) < 1).astype(jnp.int32), jax.random.fold_in(key_of[5], 1), 0, 1),
        "block_order": jax.random.permutation(key_of[6], BLOCKS).astype(jnp.int32),
    }


def reference(state, obs_tile, obs_offset, obs_value, obs_error, loc_mask, block_order):
    highest = lax.Precision.HIGHEST
    x_field = state
    for k in range(BLOCKS):
        b = block_order[k]
        start = (obs_tile[b] * TILE).astype(jnp.int32)
        slab = lax.dynamic_slice_in_dim(x_field, start, TILE, 1)
        prior = jnp.take(slab, obs_offset[b], axis=1)
        ybar = lax.optimization_barrier(jnp.mean(prior, axis=0))
        dev = prior - ybar
        var = lax.optimization_barrier(jnp.sum(dev * dev, axis=0)) / (MEMBERS - 1.0)
        error = obs_error[b]
        dy_inc = var / (var + error) * (obs_value[b] - ybar) + (jnp.sqrt(error / (var + error)) - 1.0) * dev
        weighted = dev / ((MEMBERS - 1.0) * (var + 1e-05))
        folded = jnp.dot(dy_inc, weighted.T, precision=highest)
        anom = x_field - lax.optimization_barrier(jnp.mean(x_field, axis=0))
        incr = jnp.dot(folded, anom, precision=highest)
        cols = jnp.repeat(loc_mask[b].astype(jnp.float32), TILE)
        x_field = x_field + incr * cols
    return x_field
```

```python
import jax
import jax.numpy as jnp
from jax import lax
from jax.experimental import pallas as pl
from jax.experimental.pallas import tpu as pltpu
from jax.sharding import PartitionSpec as P

MESH = pl.DeviceIdType.MESH
F32, BF16 = jnp.float32, jnp.bfloat16

MEM = 8
GX, GY = 4, 4
ROWS = 10
M = MEM * ROWS
OBS = 256
BLOCKS = 4
TILE = 128
QUAD = 4
CHUNKS = 4
QUADS = 2
WIDTH = QUADS * QUAD * TILE
OWN = CHUNKS * WIDTH
LOCAL = MEM * OWN
KDIM = 256


def split(x):
    hi = x.astype(BF16)
    lo = (x - hi.astype(F32)).astype(BF16)
    return hi, lo


def stacked(x):
    hi, lo = split(x)
    return jnp.concatenate([hi, lo, hi, jnp.zeros((KDIM - 3 * M, x.shape[1]), BF16)], axis=0)


def left_form(tri):
    hi, lo = split(tri)
    lane = lax.broadcasted_iota(jnp.int32, tri.shape, 1)
    return jnp.where(lane < 2 * M, hi.astype(F32), lo.astype(F32)).astype(BF16)


def dot(a, b):
    return jnp.dot(a, b, preferred_element_type=F32)


def dot_nt(a, b):
    return lax.dot_general(a, b, (((1,), (1,)), ((), ())), preferred_element_type=F32)


def pairs_transposed(regs):
    pair = lax.broadcasted_iota(jnp.int32, (8, TILE), 0) // 2
    out = []
    for j in range(QUAD):
        acc = None
        for i in range(QUAD):
            moved = regs[i] if i == j else pltpu.roll(regs[i], (2 * (i - j)) % 8, 0)
            acc = moved if acc is None else jnp.where(pair == i, moved, acc)
        out.append(acc)
    return out


def gathered_quad(load):
    tails = [pairs_transposed([load(4 * h + s, QUAD) for s in range(4)]) for h in range(2)]
    tiles = []
    for t in range(QUAD):
        tiles.append(jnp.concatenate([load(s, t) for s in range(MEM)] + [tails[0][t], tails[1][t]], axis=0))
    return tiles


def kernel(
    x_hbm, tile_ref, order_ref, off_ref, val_ref, err_ref, mask_ref,
    out_hbm,
    x_v, o_v, send1, recv1, send2, recv2, slab_a, slab_b, slab_c, got_x, got_y, got_m, hc, amat,
    x_sem, o_sem, ssem1, rsem1, ssem2, rsem2, xs, xr, ys, yr, ms, mr,
):
    me = lax.axis_index("mem")
    g = lax.axis_index("grid")
    gx, gy = g // GY, lax.rem(g, GY)

    load_x = pltpu.make_async_copy(x_hbm, x_v, x_sem)
    load_x.start()

    def remote(src, dst, s, r, peer):
        return pltpu.make_async_remote_copy(
            src_ref=src, dst_ref=dst, send_sem=s, recv_sem=r, device_id=peer, device_id_type=MESH
        )

    mem_peers = [{"mem": lax.rem(me + k, MEM)} for k in range(1, MEM)]
    x_peers = [{"grid": lax.rem(gx + k, GX) * GY + gy} for k in range(1, GX)]
    y_peers = [{"grid": gx * GY + lax.rem(gy + k, GY)} for k in range(1, GY)]
    barrier = pltpu.get_barrier_semaphore()
    for peer in mem_peers + x_peers + y_peers:
        pl.semaphore_signal(barrier, inc=1, device_id=peer, device_id_type=MESH)

    load_x.wait()

    blocks = [order_ref[k] for k in range(BLOCKS)]
    tiles = [tile_ref[blocks[k]] for k in range(BLOCKS)]
    per = LOCAL // TILE
    for k in range(BLOCKS):
        within = lax.rem(tiles[k], per)
        start = within * TILE
        away = tiles[k] - within - g * per
        mine = jnp.full((8, TILE), away, jnp.int32) == 0
        slab_a[k] = jnp.where(mine, x_v[0:8, pl.ds(start, TILE)], 0.0)
        slab_a[QUAD, 2 * k : 2 * k + 2, :] = jnp.where(mine[0:2], x_v[8:10, pl.ds(start, TILE)], 0.0)

    def pack(q):
        def step(d, c):
            for u in range(QUADS):
                for t in range(QUAD):
                    col = pl.multiple_of(d * OWN + q * WIDTH + (u * QUAD + t) * TILE, TILE)
                    send1[d, q, u, t] = x_v[0:8, pl.ds(col, TILE)]
                    send1[d, q, u, QUAD, 2 * t : 2 * t + 2, :] = x_v[8:10, pl.ds(col, TILE)]
            return c

        lax.fori_loop(0, MEM, step, 0)

    def out1(q, k):
        peer = mem_peers[k]
        return remote(send1.at[peer["mem"], q], recv1.at[me, q], ssem1.at[q, k], rsem1.at[q, k], peer)

    def push(q):
        for k in range(MEM - 1):
            out1(q, k).start()

    pack(0)
    pl.semaphore_wait(barrier, MEM - 1 + GX - 1 + GY - 1)

    cx = [remote(slab_a, got_x.at[k], xs.at[k], xr.at[k], x_peers[k]) for k in range(GX - 1)]
    for c in cx:
        c.start()
    push(0)
    pack(1)
    push(1)
    for c in cx:
        c.wait()
    slab_b[...] = slab_a[...] + got_x[0] + got_x[1] + got_x[2]
    cy = [remote(slab_b, got_y.at[k], ys.at[k], yr.at[k], y_peers[k]) for k in range(GY - 1)]
    for c in cy:
        c.start()
    pack(2)
    push(2)
    for c in cy:
        c.wait()
    slab_c[...] = slab_b[...] + got_y[0] + got_y[1] + got_y[2]
    cm = [remote(slab_c, got_m.at[me], ms.at[k], mr.at[k], mem_peers[k]) for k in range(MEM - 1)]
    for c in cm:
        c.start()
    got_m[me] = slab_c[...]
    pack(3)
    push(3)
    for c in cm:
        c.wait()

    slabs = gathered_quad(lambda s, t: got_m[s, t])
    lane = lax.broadcasted_iota(jnp.int32, (M, KDIM), 1)
    row = lax.broadcasted_iota(jnp.int32, (M, KDIM), 0)
    eye = jnp.where(lax.rem(lane, M) == row, 1.0, 0.0).astype(F32)
    amat[0] = eye
    hc[0] = jnp.zeros((M, KDIM), BF16)
    for k in range(BLOCKS):
        b = blocks[k]
        off = off_ref[pl.ds(b, 1), :]
        val = val_ref[pl.ds(b, 1), :]
        err = err_ref[pl.ds(b, 1), :]
        sublane = lax.broadcasted_iota(jnp.int32, (TILE, OBS), 0)
        hot = jnp.where(sublane == off, 1.0, 0.0).astype(BF16)
        top, rest = split(slabs[k])
        low = (slabs[k] - top.astype(F32) - rest.astype(F32)).astype(BF16)
        prior = dot(top, hot) + (dot(rest, hot) + dot(low, hot))
        ybar = jnp.sum(prior, axis=0, keepdims=True) * (1.0 / M)
        dev = prior - ybar
        var = jnp.sum(dev * dev, axis=0, keepdims=True) * (1.0 / (M - 1.0))
        total = var + err
        lead = var / total * (val - ybar)
        shrink = jnp.sqrt(err / total) - 1.0
        dy = lead + shrink * dev
        weighted = dev * (1.0 / ((M - 1.0) * (var + 1e-05)))
        dh, dl = split(dy)
        wh, wl = split(weighted)
        pad = jnp.zeros((KDIM - 3 * M, OBS), BF16)
        wh = jnp.concatenate([wh, wh, wh, pad], axis=0)
        wl = jnp.concatenate([wl, wl, wl, pad], axis=0)
        tri = dot_nt(dh, wh) + (dot_nt(dh, wl) + dot_nt(dl, wh))
        left = left_form(tri)
        for j in range(k + 1, BLOCKS):
            on = mask_ref[b, tiles[j]].astype(F32)
            slabs[j] = slabs[j] + on * dot(left, stacked(slabs[j]))
        for p in range(1 << k):
            base = amat[p]
            new = base + (tri if p == 0 else dot(left, stacked(base)))
            if k < BLOCKS - 1:
                amat[(1 << k) + p] = new
            hc[(1 << k) + p] = left_form(new - eye)

    def out2(q, k):
        peer = mem_peers[k]
        return remote(send2.at[peer["mem"], q], recv2.at[me, q], ssem2.at[q, k], rsem2.at[q, k], peer)

    first_tile = g * per + me * (OWN // TILE)

    def own_copy(q, c):
        recv1[me, q] = send1[me, q]
        return c

    lax.fori_loop(0, CHUNKS, own_copy, 0)

    def update(q, c):
        for k in range(MEM - 1):
            out1(q, k).wait()
        for u in range(QUADS):
            xs_ = gathered_quad(lambda s, t: recv1[s, q, u, t])
            tails = [[], []]
            for t in range(QUAD):
                tile = first_tile + q * (QUADS * QUAD) + (u * QUAD + t)
                pattern = jnp.int32(0)
                for k in range(BLOCKS):
                    pattern = pattern + mask_ref[blocks[k], tile] * (1 << k)
                y = xs_[t] + dot(hc[pattern], stacked(xs_[t]))
                for d in range(MEM):
                    send2[d, q, u, t] = y[8 * d : 8 * d + 8]
                for h in range(2):
                    tails[h].append(y[8 * MEM + 8 * h : 8 * MEM + 8 * h + 8])
            for h in range(2):
                back = pairs_transposed(tails[h])
                for d in range(4):
                    send2[4 * h + d, q, u, QUAD] = back[d]
        for k in range(MEM - 1):
            out2(q, k).start()
        recv2[me, q] = send2[me, q]
        return c

    lax.fori_loop(0, CHUNKS, update, 0)

    def finish(q, c):
        for k in range(MEM - 1):
            out2(q, k).wait()

        def step(d, c):
            for u in range(QUADS):
                for t in range(QUAD):
                    col = pl.multiple_of(d * OWN + q * WIDTH + (u * QUAD + t) * TILE, TILE)
                    o_v[0:8, pl.ds(col, TILE)] = recv2[d, q, u, t]
                    o_v[8:10, pl.ds(col, TILE)] = recv2[d, q, u, QUAD, 2 * t : 2 * t + 2, :]
            return c

        lax.fori_loop(0, MEM, step, 0)
        return c

    lax.fori_loop(0, CHUNKS, finish, 0)
    store = pltpu.make_async_copy(o_v, out_hbm, o_sem)
    store.start()
    store.wait()


def on_device(state, obs_tile, obs_offset, obs_value, obs_error, loc_mask, block_order):
    piece = (QUADS, QUAD + 1, 8, TILE)
    whole = (MEM, CHUNKS) + piece
    slab = (QUAD + 1, 8, TILE)
    smem = pl.BlockSpec(memory_space=pltpu.SMEM)
    vmem = pl.BlockSpec(memory_space=pltpu.VMEM)
    anyw = pl.BlockSpec(memory_space=pl.ANY)
    dma = pltpu.SemaphoreType.DMA
    return pl.pallas_call(
        kernel,
        out_shape=jax.ShapeDtypeStruct(state.shape, F32),
        in_specs=[anyw, smem, smem, vmem, vmem, vmem, smem],
        out_specs=anyw,
        scratch_shapes=[
            pltpu.VMEM((ROWS, LOCAL), F32),
            pltpu.VMEM((ROWS, LOCAL), F32),
            pltpu.VMEM(whole, F32),
            pltpu.VMEM(whole, F32),
            pltpu.VMEM(whole, F32),
            pltpu.VMEM(whole, F32),
            pltpu.VMEM(slab, F32),
            pltpu.VMEM(slab, F32),
            pltpu.VMEM(slab, F32),
            pltpu.VMEM((GX - 1,) + slab, F32),
            pltpu.VMEM((GY - 1,) + slab, F32),
            pltpu.VMEM((MEM,) + slab, F32),
            pltpu.VMEM((1 << BLOCKS, M, KDIM), BF16),
            pltpu.VMEM((1 << (BLOCKS - 1), M, KDIM), F32),
            dma, dma,
            dma((CHUNKS, MEM - 1)), dma((CHUNKS, MEM - 1)),
            dma((CHUNKS, MEM - 1)), dma((CHUNKS, MEM - 1)),
            dma((GX - 1,)), dma((GX - 1,)),
            dma((GY - 1,)), dma((GY - 1,)),
            dma((MEM - 1,)), dma((MEM - 1,)),
        ],
        compiler_params=pltpu.CompilerParams(
            collective_id=0, has_side_effects=True, vmem_limit_bytes=40 << 20
        ),
        name="ensemble_update",
    )(state, obs_tile, block_order, obs_offset, obs_value, obs_error, loc_mask)


def solution(mesh):
    placed = (P("mem", "grid"), P(), P(), P(), P(), P(), P())
    return jax.shard_map(
        on_device, mesh=mesh, in_specs=placed, out_specs=P("mem", "grid"), check_vma=False
    )
```

```python
import jax
import jax.numpy as jnp
from jax import lax
from jax.experimental import pallas as pl
from jax.experimental.pallas import tpu as pltpu
from jax.sharding import PartitionSpec as P

MESH = pl.DeviceIdType.MESH
F32, BF16 = jnp.float32, jnp.bfloat16

MEM = 8
GX, GY = 4, 4
ROWS = 10
M = MEM * ROWS
OBS = 256
BLOCKS = 4
TILE = 128
QUAD = 4
CHUNKS = 4
QUADS = 2
WIDTH = QUADS * QUAD * TILE
OWN = CHUNKS * WIDTH
LOCAL = MEM * OWN
PACKED = WIDTH + QUADS * TILE
KDIM = 256


def split(x):
    hi = x.astype(BF16)
    lo = (x - hi.astype(F32)).astype(BF16)
    return hi, lo


def stacked(x):
    hi, lo = split(x)
    return jnp.concatenate([hi, lo, hi, jnp.zeros((KDIM - 3 * M, x.shape[1]), BF16)], axis=0)


def left_form(tri):
    hi, lo = split(tri)
    lane = lax.broadcasted_iota(jnp.int32, tri.shape, 1)
    return jnp.where(lane < 2 * M, hi.astype(F32), lo.astype(F32)).astype(BF16)


def dot(a, b):
    return jnp.dot(a, b, preferred_element_type=F32)


def dot_nt(a, b):
    return lax.dot_general(a, b, (((1,), (1,)), ((), ())), preferred_element_type=F32)


def pairs_transposed(regs):
    pair = lax.broadcasted_iota(jnp.int32, (8, TILE), 0) // 2
    out = []
    for j in range(QUAD):
        acc = None
        for i in range(QUAD):
            moved = regs[i] if i == j else pltpu.roll(regs[i], (2 * (i - j)) % 8, 0)
            acc = moved if acc is None else jnp.where(pair == i, moved, acc)
        out.append(acc)
    return out


def gathered_quad(main, tail):
    tails = [pairs_transposed([tail(4 * h + s) for s in range(4)]) for h in range(2)]
    tiles = []
    for t in range(QUAD):
        tiles.append(jnp.concatenate([main(s, t) for s in range(MEM)] + [tails[0][t], tails[1][t]], axis=0))
    return tiles


def lanes(tile):
    return pl.ds(tile * TILE, TILE)


def kernel(
    x_hbm, tile_hbm, order_hbm, off_hbm, val_hbm, err_hbm, mask_hbm,
    recv2,
    x_v, tile_ref, order_ref, off_ref, val_ref, err_ref, mask_ref,
    tails, recv1, send2, slab_a, slab_b, slab_c, got_x, got_y, got_m, hc, amat,
    x_sem, in_sem, own_sem, ssem1, rsem1, tsend, trecv, ssem2, rsem2, xs, xr, ys, yr, ms, mr,
):
    me = lax.axis_index("mem")
    g = lax.axis_index("grid")
    gx, gy = g // GY, lax.rem(g, GY)

    def remote(src, dst, s, r, peer):
        return pltpu.make_async_remote_copy(
            src_ref=src, dst_ref=dst, send_sem=s, recv_sem=r, device_id=peer, device_id_type=MESH
        )

    mem_peers = [{"mem": lax.rem(me + k, MEM)} for k in range(1, MEM)]
    x_peers = [{"grid": lax.rem(gx + k, GX) * GY + gy} for k in range(1, GX)]
    y_peers = [{"grid": gx * GY + lax.rem(gy + k, GY)} for k in range(1, GY)]
    barrier = pltpu.get_barrier_semaphore()
    for peer in mem_peers + x_peers + y_peers:
        pl.semaphore_signal(barrier, inc=1, device_id=peer, device_id_type=MESH)

    small = [
        pltpu.make_async_copy(src, dst, in_sem.at[i])
        for i, (src, dst) in enumerate([
            (order_hbm, order_ref), (tile_hbm, tile_ref), (mask_hbm, mask_ref),
            (off_hbm, off_ref), (val_hbm, val_ref), (err_hbm, err_ref),
        ])
    ]
    load_x = pltpu.make_async_copy(x_hbm, x_v, x_sem)
    load_x.start()
    for c in small:
        c.start()

    def columns(d, q):
        return pl.ds(pl.multiple_of(d * OWN + q * WIDTH, WIDTH), WIDTH)

    def out1(q, k):
        peer = mem_peers[k]
        src = x_hbm.at[0:8, columns(peer["mem"], q)]
        return remote(src, recv1.at[me, q, :, 0:WIDTH], ssem1.at[q, k], rsem1.at[q, k], peer)

    def out_tails(k):
        peer = mem_peers[k]
        dst = recv1.at[me, :, :, WIDTH:PACKED]
        return remote(tails.at[peer["mem"]], dst, tsend.at[k], trecv.at[k], peer)

    def push(q):
        for k in range(MEM - 1):
            out1(q, k).start()

    for c in small:
        c.wait()
    load_x.wait()

    blocks = [order_ref[k] for k in range(BLOCKS)]
    tiles = [tile_ref[blocks[k]] for k in range(BLOCKS)]
    per = LOCAL // TILE
    for k in range(BLOCKS):
        within = lax.rem(tiles[k], per)
        start = within * TILE
        away = tiles[k] - within - g * per
        mine = jnp.full((8, TILE), away, jnp.int32) == 0
        slab_a[k] = jnp.where(mine, x_v[0:8, pl.ds(start, TILE)], 0.0)
        slab_a[QUAD, 2 * k : 2 * k + 2, :] = jnp.where(mine[0:2], x_v[8:10, pl.ds(start, TILE)], 0.0)

    pl.semaphore_wait(barrier, MEM - 1 + GX - 1 + GY - 1)

    cx = [remote(slab_a, got_x.at[k], xs.at[k], xr.at[k], x_peers[k]) for k in range(GX - 1)]
    for c in cx:
        c.start()
    push(0)

    def pack(d, c):
        for q in range(CHUNKS):
            for u in range(QUADS):
                for t in range(QUAD):
                    col = pl.multiple_of(d * OWN + q * WIDTH + (u * QUAD + t) * TILE, TILE)
                    tails[d, q, 2 * t : 2 * t + 2, u * TILE : (u + 1) * TILE] = x_v[8:10, pl.ds(col, TILE)]
        return c

    lax.fori_loop(0, MEM, pack, 0)
    for c in cx:
        c.wait()
    slab_b[...] = slab_a[...] + got_x[0] + got_x[1] + got_x[2]
    cy = [remote(slab_b, got_y.at[k], ys.at[k], yr.at[k], y_peers[k]) for k in range(GY - 1)]
    for c in cy:
        c.start()
    for k in range(MEM - 1):
        out_tails(k).start()
    for c in cy:
        c.wait()
    slab_c[...] = slab_b[...] + got_y[0] + got_y[1] + got_y[2]
    cm = [remote(slab_c, got_m.at[me], ms.at[k], mr.at[k], mem_peers[k]) for k in range(MEM - 1)]
    for c in cm:
        c.start()
    got_m[me] = slab_c[...]
    for q in range(1, CHUNKS):
        push(q)
    own = [
        pltpu.make_async_copy(x_hbm.at[0:8, columns(me, q)], recv1.at[me, q, :, 0:WIDTH], own_sem.at[q])
        for q in range(CHUNKS)
    ]
    for c in own:
        c.start()
    recv1[me, :, :, WIDTH:PACKED] = tails[me]
    for c in cm:
        c.wait()

    slabs = gathered_quad(lambda s, t: got_m[s, t], lambda s: got_m[s, QUAD])
    lane = lax.broadcasted_iota(jnp.int32, (M, KDIM), 1)
    row = lax.broadcasted_iota(jnp.int32, (M, KDIM), 0)
    eye = jnp.where(lax.rem(lane, M) == row, 1.0, 0.0).astype(F32)
    amat[0] = eye
    hc[0] = jnp.zeros((M, KDIM), BF16)
    for k in range(BLOCKS):
        b = blocks[k]
        off = off_ref[pl.ds(b, 1), :]
        val = val_ref[pl.ds(b, 1), :]
        err = err_ref[pl.ds(b, 1), :]
        sublane = lax.broadcasted_iota(jnp.int32, (TILE, OBS), 0)
        hot = jnp.where(sublane == off, 1.0, 0.0).astype(BF16)
        top, rest = split(slabs[k])
        low = (slabs[k] - top.astype(F32) - rest.astype(F32)).astype(BF16)
        prior = dot(top, hot) + (dot(rest, hot) + dot(low, hot))
        ybar = jnp.sum(prior, axis=0, keepdims=True) * (1.0 / M)
        dev = prior - ybar
        var = jnp.sum(dev * dev, axis=0, keepdims=True) * (1.0 / (M - 1.0))
        total = var + err
        lead = var / total * (val - ybar)
        shrink = jnp.sqrt(err / total) - 1.0
        dy = lead + shrink * dev
        weighted = dev * (1.0 / ((M - 1.0) * (var + 1e-05)))
        dh, dl = split(dy)
        wh, wl = split(weighted)
        pad = jnp.zeros((KDIM - 3 * M, OBS), BF16)
        wh = jnp.concatenate([wh, wh, wh, pad], axis=0)
        wl = jnp.concatenate([wl, wl, wl, pad], axis=0)
        tri = dot_nt(dh, wh) + (dot_nt(dh, wl) + dot_nt(dl, wh))
        left = left_form(tri)
        for j in range(k + 1, BLOCKS):
            on = mask_ref[b, tiles[j]].astype(F32)
            slabs[j] = slabs[j] + on * dot(left, stacked(slabs[j]))
        for p in range(1 << k):
            base = amat[p]
            new = base + (tri if p == 0 else dot(left, stacked(base)))
            if k < BLOCKS - 1:
                amat[(1 << k) + p] = new
            hc[(1 << k) + p] = left_form(new - eye)

    for c in own:
        c.wait()
    for k in range(MEM - 1):
        out_tails(k).wait()

    def out2(q, k):
        peer = mem_peers[k]
        return remote(send2.at[peer["mem"], q], recv2.at[me, q], ssem2.at[q, k], rsem2.at[q, k], peer)

    def keep(q):
        return pltpu.make_async_copy(send2.at[me, q], recv2.at[me, q], own_sem.at[q])

    first_tile = g * per + me * (OWN // TILE)

    def update(q, c):
        for k in range(MEM - 1):
            out1(q, k).wait()
        for u in range(QUADS):
            quad = gathered_quad(
                lambda s, t: recv1[s, q, :, lanes(u * QUAD + t)], lambda s: recv1[s, q, :, lanes(QUADS * QUAD + u)]
            )
            pairs = [[], []]
            for t in range(QUAD):
                tile = first_tile + q * (QUADS * QUAD) + (u * QUAD + t)
                pattern = jnp.int32(0)
                for k in range(BLOCKS):
                    pattern = pattern + mask_ref[blocks[k], tile] * (1 << k)
                y = quad[t] + dot(hc[pattern], stacked(quad[t]))
                for d in range(MEM):
                    send2[d, q, :, lanes(u * QUAD + t)] = y[8 * d : 8 * d + 8]
                for h in range(2):
                    pairs[h].append(y[8 * MEM + 8 * h : 8 * MEM + 8 * h + 8])
            for h in range(2):
                back = pairs_transposed(pairs[h])
                for d in range(4):
                    send2[4 * h + d, q, :, lanes(QUADS * QUAD + u)] = back[d]
        for k in range(MEM - 1):
            out2(q, k).start()
        keep(q).start()
        return c

    lax.fori_loop(0, CHUNKS, update, 0)
    for q in range(CHUNKS):
        keep(q).wait()
        for k in range(MEM - 1):
            out2(q, k).wait()


def unpack(packed, out, held, rows_v, in_sem, main_sem, row_sem):
    loads = [pltpu.make_async_copy(packed.at[d], held.at[d], in_sem.at[d]) for d in range(MEM)]
    for c in loads:
        c.start()
    started = []
    for d in range(MEM):
        loads[d].wait()
        for q in range(CHUNKS):
            cols = pl.ds(d * OWN + q * WIDTH, WIDTH)
            started.append(pltpu.make_async_copy(held.at[d, q, :, 0:WIDTH], out.at[0:8, cols], main_sem.at[d, q]))
            started[-1].start()
        for q in range(CHUNKS):
            for u in range(QUADS):
                for t in range(QUAD):
                    col = d * OWN + q * WIDTH + (u * QUAD + t) * TILE
                    rows_v[:, col : col + TILE] = held[d, q, 2 * t : 2 * t + 2, WIDTH + u * TILE : WIDTH + (u + 1) * TILE]
        cols = pl.ds(d * OWN, OWN)
        started.append(pltpu.make_async_copy(rows_v.at[:, cols], out.at[8:10, cols], row_sem.at[d]))
        started[-1].start()
    for c in started:
        c.wait()


def on_device(state, obs_tile, obs_offset, obs_value, obs_error, loc_mask, block_order):
    whole = (MEM, CHUNKS, 8, PACKED)
    slab = (QUAD + 1, 8, TILE)
    hbm = pl.BlockSpec(memory_space=pltpu.HBM)
    dma = pltpu.SemaphoreType.DMA
    packed = pl.pallas_call(
        kernel,
        out_shape=jax.ShapeDtypeStruct(whole, F32),
        in_specs=[hbm] * 7,
        out_specs=hbm,
        scratch_shapes=[
            pltpu.VMEM((ROWS, LOCAL), F32),
            pltpu.SMEM((BLOCKS,), jnp.int32),
            pltpu.SMEM((BLOCKS,), jnp.int32),
            pltpu.VMEM((BLOCKS, OBS), jnp.int32),
            pltpu.VMEM((BLOCKS, OBS), F32),
            pltpu.VMEM((BLOCKS, OBS), F32),
            pltpu.SMEM((BLOCKS, GX * GY * LOCAL // TILE), jnp.int32),
            pltpu.VMEM((MEM, CHUNKS, 8, QUADS * TILE), F32),
            pltpu.VMEM(whole, F32),
            pltpu.VMEM(whole, F32),
            pltpu.VMEM(slab, F32),
            pltpu.VMEM(slab, F32),
            pltpu.VMEM(slab, F32),
            pltpu.VMEM((GX - 1,) + slab, F32),
            pltpu.VMEM((GY - 1,) + slab, F32),
            pltpu.VMEM((MEM,) + slab, F32),
            pltpu.VMEM((1 << BLOCKS, M, KDIM), BF16),
            pltpu.VMEM((1 << (BLOCKS - 1), M, KDIM), F32),
            dma, dma((6,)), dma((CHUNKS,)),
            dma((CHUNKS, MEM - 1)), dma((CHUNKS, MEM - 1)),
            dma((MEM - 1,)), dma((MEM - 1,)),
            dma((CHUNKS, MEM - 1)), dma((CHUNKS, MEM - 1)),
            dma((GX - 1,)), dma((GX - 1,)),
            dma((GY - 1,)), dma((GY - 1,)),
            dma((MEM - 1,)), dma((MEM - 1,)),
        ],
        compiler_params=pltpu.CompilerParams(
            collective_id=0, has_side_effects=True, vmem_limit_bytes=64 << 20
        ),
        name="ensemble_update",
    )(state, obs_tile, block_order, obs_offset, obs_value, obs_error, loc_mask)
    return pl.pallas_call(
        unpack,
        out_shape=jax.ShapeDtypeStruct(state.shape, F32),
        in_specs=[hbm],
        out_specs=hbm,
        scratch_shapes=[
            pltpu.VMEM(whole, F32),
            pltpu.VMEM((ROWS - 8, LOCAL), F32),
            dma((MEM,)), dma((MEM, CHUNKS)), dma((MEM,)),
        ],
        compiler_params=pltpu.CompilerParams(vmem_limit_bytes=64 << 20),
        name="unpack",
    )(packed)


def solution(mesh):
    placed = (P("mem", "grid"), P(), P(), P(), P(), P(), P())
    return jax.shard_map(
        on_device, mesh=mesh, in_specs=placed, out_specs=P("mem", "grid"), check_vma=False
    )
```

```python
import jax
import jax.numpy as jnp
from jax import lax
from jax.experimental import pallas as pl
from jax.experimental.pallas import tpu as pltpu
from jax.sharding import PartitionSpec as P

MESH = pl.DeviceIdType.MESH
F32, BF16 = jnp.float32, jnp.bfloat16

MEM = 8
GX, GY = 4, 4
ROWS = 10
M = MEM * ROWS
OBS = 256
BLOCKS = 4
TILE = 128
QUAD = 4
CHUNKS = 2
QUADS = 4
WIDTH = QUADS * QUAD * TILE
OWN = CHUNKS * WIDTH
LOCAL = MEM * OWN
PACKED = WIDTH + QUADS * TILE
DEPTH = 21
LOADS = 4
HOPS = [(1, 0), (3, 0), (2, 1), (1, 1), (3, 1), (2, 0), (0, 1)]
KDIM = 256


def split(x):
    hi = x.astype(BF16)
    lo = (x - hi.astype(F32)).astype(BF16)
    return hi, lo


def stacked(x):
    hi, lo = split(x)
    return jnp.concatenate([hi, lo, hi, jnp.zeros((KDIM - 3 * M, x.shape[1]), BF16)], axis=0)


def left_form(tri):
    hi, lo = split(tri)
    lane = lax.broadcasted_iota(jnp.int32, tri.shape, 1)
    return jnp.where(lane < 2 * M, hi.astype(F32), lo.astype(F32)).astype(BF16)


def dot(a, b):
    return jnp.dot(a, b, preferred_element_type=F32)


def dot_nt(a, b):
    return lax.dot_general(a, b, (((1,), (1,)), ((), ())), preferred_element_type=F32)


def pairs_transposed(regs):
    pair = lax.broadcasted_iota(jnp.int32, (8, TILE), 0) // 2
    out = []
    for j in range(QUAD):
        acc = None
        for i in range(QUAD):
            moved = regs[i] if i == j else pltpu.roll(regs[i], (2 * (i - j)) % 8, 0)
            acc = moved if acc is None else jnp.where(pair == i, moved, acc)
        out.append(acc)
    return out


def gathered_quad(main, tail):
    tails = [pairs_transposed([tail(4 * h + s) for s in range(4)]) for h in range(2)]
    tiles = []
    for t in range(QUAD):
        tiles.append(jnp.concatenate([main(s, t) for s in range(MEM)] + [tails[0][t], tails[1][t]], axis=0))
    return tiles


def lanes(tile):
    return pl.ds(tile * TILE, TILE)


def kernel(
    x_hbm, tile_hbm, order_hbm, off_hbm, val_hbm, err_hbm, mask_hbm,
    recv2,
    x_v, tile_ref, order_ref, off_ref, val_ref, err_ref, mask_ref,
    tails, recv1, send2, slab_a, slab_b, slab_c, got_x, got_y, got_m, hc, amat,
    x_sem, in_sem, own_sem, ssem1, rsem1, tsend, trecv, ssem2, rsem2, xs, xr, ys, yr, ms, mr,
):
    me = lax.axis_index("mem")
    g = lax.axis_index("grid")
    gx, gy = g // GY, lax.rem(g, GY)

    def remote(src, dst, s, r, peer):
        return pltpu.make_async_remote_copy(
            src_ref=src, dst_ref=dst, send_sem=s, recv_sem=r, device_id=peer, device_id_type=MESH
        )

    z, core = me // 2, lax.rem(me, 2)
    mem_peers = [{"mem": lax.rem(z + dz, MEM // 2) * 2 + lax.rem(core + dc, 2)} for dz, dc in HOPS]
    x_peers = [{"grid": lax.rem(gx + k, GX) * GY + gy} for k in range(1, GX)]
    y_peers = [{"grid": gx * GY + lax.rem(gy + k, GY)} for k in range(1, GY)]
    barrier = pltpu.get_barrier_semaphore()
    for peer in mem_peers + x_peers + y_peers:
        pl.semaphore_signal(barrier, inc=1, device_id=peer, device_id_type=MESH)

    small = [
        pltpu.make_async_copy(src, dst, in_sem.at[i])
        for i, (src, dst) in enumerate([
            (order_hbm, order_ref), (tile_hbm, tile_ref), (mask_hbm, mask_ref),
            (off_hbm, off_ref), (val_hbm, val_ref), (err_hbm, err_ref),
        ])
    ]
    load_x = []
    for i in range(LOADS):
        cols = pl.ds(i * (LOCAL // LOADS), LOCAL // LOADS)
        load_x.append(pltpu.make_async_copy(x_hbm.at[:, cols], x_v.at[:, cols], x_sem.at[i]))
    for c in small[:2] + load_x + small[2:]:
        c.start()

    def columns(d, q):
        return pl.ds(pl.multiple_of(d * OWN + q * WIDTH, WIDTH), WIDTH)

    def out1(q, k):
        peer = mem_peers[k]
        src = x_hbm.at[0:8, columns(peer["mem"], q)]
        return remote(src, recv1.at[me, q, :, 0:WIDTH], ssem1.at[q, k], rsem1.at[q, k], peer)

    def out_tails(k):
        peer = mem_peers[k]
        dst = recv1.at[me, :, :, WIDTH:PACKED]
        return remote(tails.at[peer["mem"]], dst, tsend.at[k], trecv.at[k], peer)

    pieces = [out1(q, k) for q in range(CHUNKS) for k in range(MEM - 1)]
    pieces[7:7] = [out_tails(k) for k in range(MEM - 1)]

    def feed(upto):
        while fed[0] < upto:
            if fed[0] >= DEPTH:
                pieces[fed[0] - DEPTH].wait_send()
            pieces[fed[0]].start()
            fed[0] += 1

    fed = [0]
    for c in small[:2] + load_x:
        c.wait()

    blocks = [order_ref[k] for k in range(BLOCKS)]
    tiles = [tile_ref[blocks[k]] for k in range(BLOCKS)]
    per = LOCAL // TILE
    for k in range(BLOCKS):
        within = lax.rem(tiles[k], per)
        start = within * TILE
        away = tiles[k] - within - g * per
        mine = jnp.full((8, TILE), away, jnp.int32) == 0
        slab_a[k] = jnp.where(mine, x_v[0:8, pl.ds(start, TILE)], 0.0)
        slab_a[QUAD, 2 * k : 2 * k + 2, :] = jnp.where(mine[0:2], x_v[8:10, pl.ds(start, TILE)], 0.0)

    pl.semaphore_wait(barrier, MEM - 1 + GX - 1 + GY - 1)

    cx = [remote(slab_a, got_x.at[k], xs.at[k], xr.at[k], x_peers[k]) for k in range(GX - 1)]
    for c in cx:
        c.start()
    feed(7)

    def pack(d, c):
        for q in range(CHUNKS):
            for u in range(QUADS):
                for t in range(QUAD):
                    col = pl.multiple_of(d * OWN + q * WIDTH + (u * QUAD + t) * TILE, TILE)
                    tails[d, q, 2 * t : 2 * t + 2, u * TILE : (u + 1) * TILE] = x_v[8:10, pl.ds(col, TILE)]
        return c

    lax.fori_loop(0, MEM, pack, 0)
    own = [
        pltpu.make_async_copy(x_hbm.at[0:8, columns(me, q)], recv1.at[me, q, :, 0:WIDTH], own_sem.at[q])
        for q in range(CHUNKS)
    ]
    for c in own:
        c.start()
    recv1[me, :, :, WIDTH:PACKED] = tails[me]
    feed(7)
    for c in cx:
        c.wait()
    slab_b[...] = slab_a[...] + got_x[0] + got_x[1] + got_x[2]
    cy = [remote(slab_b, got_y.at[k], ys.at[k], yr.at[k], y_peers[k]) for k in range(GY - 1)]
    for c in cy:
        c.start()
    feed(14)
    for c in cy:
        c.wait()
    slab_c[...] = slab_b[...] + got_y[0] + got_y[1] + got_y[2]
    cm = [remote(slab_c, got_m.at[me], ms.at[k], mr.at[k], mem_peers[k]) for k in range(MEM - 1)]
    for c in cm:
        c.start()
    got_m[me] = slab_c[...]
    feed(21)
    for c in cm:
        c.wait()

    for c in small[2:]:
        c.wait()
    slabs = gathered_quad(lambda s, t: got_m[s, t], lambda s: got_m[s, QUAD])
    lane = lax.broadcasted_iota(jnp.int32, (M, KDIM), 1)
    row = lax.broadcasted_iota(jnp.int32, (M, KDIM), 0)
    eye = jnp.where(lax.rem(lane, M) == row, 1.0, 0.0).astype(F32)
    amat[0] = eye
    hc[0] = jnp.zeros((M, KDIM), BF16)
    for k in range(BLOCKS):
        b = blocks[k]
        off = off_ref[pl.ds(b, 1), :]
        val = val_ref[pl.ds(b, 1), :]
        err = err_ref[pl.ds(b, 1), :]
        sublane = lax.broadcasted_iota(jnp.int32, (TILE, OBS), 0)
        hot = jnp.where(sublane == off, 1.0, 0.0).astype(BF16)
        top, rest = split(slabs[k])
        low = (slabs[k] - top.astype(F32) - rest.astype(F32)).astype(BF16)
        prior = dot(top, hot) + (dot(rest, hot) + dot(low, hot))
        ybar = jnp.sum(prior, axis=0, keepdims=True) * (1.0 / M)
        dev = prior - ybar
        var = jnp.sum(dev * dev, axis=0, keepdims=True) * (1.0 / (M - 1.0))
        total = var + err
        lead = var / total * (val - ybar)
        shrink = jnp.sqrt(err / total) - 1.0
        dy = lead + shrink * dev
        weighted = dev * (1.0 / ((M - 1.0) * (var + 1e-05)))
        dh, dl = split(dy)
        wh, wl = split(weighted)
        pad = jnp.zeros((KDIM - 3 * M, OBS), BF16)
        wh = jnp.concatenate([wh, wh, wh, pad], axis=0)
        wl = jnp.concatenate([wl, wl, wl, pad], axis=0)
        tri = dot_nt(dh, wh) + (dot_nt(dh, wl) + dot_nt(dl, wh))
        left = left_form(tri)
        for j in range(k + 1, BLOCKS):
            on = mask_ref[b, tiles[j]].astype(F32)
            slabs[j] = slabs[j] + on * dot(left, stacked(slabs[j]))
        for p in range(1 << k):
            base = amat[p]
            new = base + (tri if p == 0 else dot(left, stacked(base)))
            if k < BLOCKS - 1:
                amat[(1 << k) + p] = new
            hc[(1 << k) + p] = left_form(new - eye)

    feed(len(pieces))
    for c in own:
        c.wait()
    for k in range(MEM - 1):
        out_tails(k).wait_recv()

    def out2(q, k):
        peer = mem_peers[k]
        return remote(send2.at[peer["mem"], q], recv2.at[me, q], ssem2.at[q, k], rsem2.at[q, k], peer)

    def keep(q):
        return pltpu.make_async_copy(send2.at[me, q], recv2.at[me, q], own_sem.at[q])

    first_tile = g * per + me * (OWN // TILE)

    def update(q, c):
        for k in range(MEM - 1):
            out1(q, k).wait_recv()
        for u in range(QUADS):
            quad = gathered_quad(
                lambda s, t: recv1[s, q, :, lanes(u * QUAD + t)], lambda s: recv1[s, q, :, lanes(QUADS * QUAD + u)]
            )
            pairs = [[], []]
            for t in range(QUAD):
                tile = first_tile + q * (QUADS * QUAD) + (u * QUAD + t)
                pattern = jnp.int32(0)
                for k in range(BLOCKS):
                    pattern = pattern + mask_ref[blocks[k], tile] * (1 << k)
                y = quad[t] + dot(hc[pattern], stacked(quad[t]))
                for d in range(MEM):
                    send2[d, q, :, lanes(u * QUAD + t)] = y[8 * d : 8 * d + 8]
                for h in range(2):
                    pairs[h].append(y[8 * MEM + 8 * h : 8 * MEM + 8 * h + 8])
            for h in range(2):
                back = pairs_transposed(pairs[h])
                for d in range(4):
                    send2[4 * h + d, q, :, lanes(QUADS * QUAD + u)] = back[d]
        for k in range(MEM - 1):
            out2(q, k).start()
        keep(q).start()
        return c

    lax.fori_loop(0, CHUNKS, update, 0)
    for q in range(CHUNKS):
        keep(q).wait()
        for k in range(MEM - 1):
            out2(q, k).wait()
    for piece in pieces[-DEPTH:]:
        piece.wait_send()


def unpack(packed, out, rows_v, main_sem, row_sem):
    started = []
    for d in range(MEM):
        for q in range(CHUNKS):
            cols = pl.ds(d * OWN + q * WIDTH, WIDTH)
            started.append(pltpu.make_async_copy(packed.at[d, q, :, 0:WIDTH], out.at[0:8, cols], main_sem.at[d, q]))
            started[-1].start()
    for d in range(MEM):
        for q in range(CHUNKS):
            for u in range(QUADS):
                for t in range(QUAD):
                    col = d * OWN + q * WIDTH + (u * QUAD + t) * TILE
                    rows_v[:, col : col + TILE] = packed[d, q, 2 * t : 2 * t + 2, WIDTH + u * TILE : WIDTH + (u + 1) * TILE]
        cols = pl.ds(d * OWN, OWN)
        started.append(pltpu.make_async_copy(rows_v.at[:, cols], out.at[8:10, cols], row_sem.at[d]))
        started[-1].start()
    for c in started:
        c.wait()


def on_device(state, obs_tile, obs_offset, obs_value, obs_error, loc_mask, block_order):
    whole = (MEM, CHUNKS, 8, PACKED)
    slab = (QUAD + 1, 8, TILE)
    hbm = pl.BlockSpec(memory_space=pltpu.HBM)
    dma = pltpu.SemaphoreType.DMA
    args = (state, obs_tile, block_order, obs_offset, obs_value, obs_error, loc_mask)
    args = [pltpu.with_memory_space_constraint(a, pltpu.HBM) for a in args]
    packed = pl.pallas_call(
        kernel,
        out_shape=jax.ShapeDtypeStruct(whole, F32),
        in_specs=[hbm] * 7,
        out_specs=hbm,
        scratch_shapes=[
            pltpu.VMEM((ROWS, LOCAL), F32),
            pltpu.SMEM((BLOCKS,), jnp.int32),
            pltpu.SMEM((BLOCKS,), jnp.int32),
            pltpu.VMEM((BLOCKS, OBS), jnp.int32),
            pltpu.VMEM((BLOCKS, OBS), F32),
            pltpu.VMEM((BLOCKS, OBS), F32),
            pltpu.SMEM((BLOCKS, GX * GY * LOCAL // TILE), jnp.int32),
            pltpu.VMEM((MEM, CHUNKS, 8, QUADS * TILE), F32),
            pltpu.VMEM(whole, F32),
            pltpu.VMEM(whole, F32),
            pltpu.VMEM(slab, F32),
            pltpu.VMEM(slab, F32),
            pltpu.VMEM(slab, F32),
            pltpu.VMEM((GX - 1,) + slab, F32),
            pltpu.VMEM((GY - 1,) + slab, F32),
            pltpu.VMEM((MEM,) + slab, F32),
            pltpu.VMEM((1 << BLOCKS, M, KDIM), BF16),
            pltpu.VMEM((1 << (BLOCKS - 1), M, KDIM), F32),
            dma((LOADS,)), dma((6,)), dma((CHUNKS,)),
            dma((CHUNKS, MEM - 1)), dma((CHUNKS, MEM - 1)),
            dma((MEM - 1,)), dma((MEM - 1,)),
            dma((CHUNKS, MEM - 1)), dma((CHUNKS, MEM - 1)),
            dma((GX - 1,)), dma((GX - 1,)),
            dma((GY - 1,)), dma((GY - 1,)),
            dma((MEM - 1,)), dma((MEM - 1,)),
        ],
        compiler_params=pltpu.CompilerParams(
            collective_id=0, has_side_effects=True, vmem_limit_bytes=40 << 20
        ),
        name="ensemble_update",
    )(*args)
    return pl.pallas_call(
        unpack,
        out_shape=jax.ShapeDtypeStruct(state.shape, F32),
        in_specs=[pl.BlockSpec(memory_space=pltpu.VMEM)],
        out_specs=hbm,
        scratch_shapes=[pltpu.VMEM((ROWS - 8, LOCAL), F32), dma((MEM, CHUNKS)), dma((MEM,))],
        compiler_params=pltpu.CompilerParams(vmem_limit_bytes=16 << 20),
        name="unpack",
    )(packed)


def solution(mesh):
    placed = (P("mem", "grid"), P(), P(), P(), P(), P(), P())
    return jax.shard_map(
        on_device, mesh=mesh, in_specs=placed, out_specs=P("mem", "grid"), check_vma=False
    )
```

```python
import jax
import jax.numpy as jnp
from jax import lax
from jax.experimental import pallas as pl
from jax.experimental.pallas import tpu as pltpu
from jax.sharding import PartitionSpec as P

MESH = pl.DeviceIdType.MESH
F32, BF16 = jnp.float32, jnp.bfloat16

MEM = 8
GX, GY = 4, 4
ROWS = 10
M = MEM * ROWS
OBS = 256
BLOCKS = 4
TILE = 128
QUAD = 4
CHUNKS = 2
QUADS = 4
WIDTH = QUADS * QUAD * TILE
OWN = CHUNKS * WIDTH
LOCAL = MEM * OWN
PACKED = WIDTH + QUADS * TILE
DEPTH = 21
LOADS = 4
HOPS = [(1, 0), (3, 0), (2, 1), (1, 1), (3, 1), (2, 0), (0, 1)]
KDIM = 256


def split(x):
    hi = x.astype(BF16)
    lo = (x - hi.astype(F32)).astype(BF16)
    return hi, lo


def stacked(x):
    hi, lo = split(x)
    return jnp.concatenate([hi, lo, hi, jnp.zeros((KDIM - 3 * M, x.shape[1]), BF16)], axis=0)


def left_form(tri):
    hi, lo = split(tri)
    lane = lax.broadcasted_iota(jnp.int32, tri.shape, 1)
    return jnp.where(lane < 2 * M, hi.astype(F32), lo.astype(F32)).astype(BF16)


def dot(a, b):
    return jnp.dot(a, b, preferred_element_type=F32)


def dot_nt(a, b):
    return lax.dot_general(a, b, (((1,), (1,)), ((), ())), preferred_element_type=F32)


def pairs_transposed(regs):
    pair = lax.broadcasted_iota(jnp.int32, (8, TILE), 0) // 2
    out = []
    for j in range(QUAD):
        acc = None
        for i in range(QUAD):
            moved = regs[i] if i == j else pltpu.roll(regs[i], (2 * (i - j)) % 8, 0)
            acc = moved if acc is None else jnp.where(pair == i, moved, acc)
        out.append(acc)
    return out


def gathered_quad(main, tail):
    tails = [pairs_transposed([tail(4 * h + s) for s in range(4)]) for h in range(2)]
    tiles = []
    for t in range(QUAD):
        tiles.append(jnp.concatenate([main(s, t) for s in range(MEM)] + [tails[0][t], tails[1][t]], axis=0))
    return tiles


def lanes(tile):
    return pl.ds(tile * TILE, TILE)


def kernel(
    x_hbm, tile_hbm, order_hbm, off_hbm, val_hbm, err_hbm, mask_hbm,
    recv2,
    x_v, tile_ref, order_ref, off_ref, val_ref, err_ref, mask_ref,
    tails, recv1, send2, slab_a, slab_b, slab_c, got_x, got_y, got_m, hc,
    x_sem, in_sem, own_sem, ssem1, rsem1, tsend, trecv, ssem2, rsem2, xs, xr, ys, yr, ms, mr,
):
    me = lax.axis_index("mem")
    g = lax.axis_index("grid")
    gx, gy = g // GY, lax.rem(g, GY)

    def remote(src, dst, s, r, peer):
        return pltpu.make_async_remote_copy(
            src_ref=src, dst_ref=dst, send_sem=s, recv_sem=r, device_id=peer, device_id_type=MESH
        )

    z, core = me // 2, lax.rem(me, 2)
    mem_peers = [{"mem": lax.rem(z + dz, MEM // 2) * 2 + lax.rem(core + dc, 2)} for dz, dc in HOPS]
    x_peers = [{"grid": lax.rem(gx + k, GX) * GY + gy} for k in range(1, GX)]
    y_peers = [{"grid": gx * GY + lax.rem(gy + k, GY)} for k in range(1, GY)]
    barrier = pltpu.get_barrier_semaphore()
    for peer in mem_peers + x_peers + y_peers:
        pl.semaphore_signal(barrier, inc=1, device_id=peer, device_id_type=MESH)

    small = [
        pltpu.make_async_copy(src, dst, in_sem.at[i])
        for i, (src, dst) in enumerate([
            (order_hbm, order_ref), (tile_hbm, tile_ref), (mask_hbm, mask_ref),
            (off_hbm, off_ref), (val_hbm, val_ref), (err_hbm, err_ref),
        ])
    ]
    load_x = []
    for i in range(LOADS):
        cols = pl.ds(i * (LOCAL // LOADS), LOCAL // LOADS)
        load_x.append(pltpu.make_async_copy(x_hbm.at[:, cols], x_v.at[:, cols], x_sem.at[i]))
    for c in small[:2] + load_x + small[2:]:
        c.start()

    def columns(d, q):
        return pl.ds(pl.multiple_of(d * OWN + q * WIDTH, WIDTH), WIDTH)

    def out1(q, k):
        peer = mem_peers[k]
        src = x_hbm.at[0:8, columns(peer["mem"], q)]
        return remote(src, recv1.at[me, q, :, 0:WIDTH], ssem1.at[q, k], rsem1.at[q, k], peer)

    def out_tails(k):
        peer = mem_peers[k]
        dst = recv1.at[me, :, :, WIDTH:PACKED]
        return remote(tails.at[peer["mem"]], dst, tsend.at[k], trecv.at[k], peer)

    pieces = [out1(q, k) for q in range(CHUNKS) for k in range(MEM - 1)]
    pieces[7:7] = [out_tails(k) for k in range(MEM - 1)]

    def feed(upto):
        while fed[0] < upto:
            if fed[0] >= DEPTH:
                pieces[fed[0] - DEPTH].wait_send()
            pieces[fed[0]].start()
            fed[0] += 1

    fed = [0]
    for c in small[:2] + load_x:
        c.wait()

    blocks = [order_ref[k] for k in range(BLOCKS)]
    tiles = [tile_ref[blocks[k]] for k in range(BLOCKS)]
    per = LOCAL // TILE
    for k in range(BLOCKS):
        within = lax.rem(tiles[k], per)
        start = within * TILE
        away = tiles[k] - within - g * per
        mine = jnp.full((8, TILE), away, jnp.int32) == 0
        slab_a[k] = jnp.where(mine, x_v[0:8, pl.ds(start, TILE)], 0.0)
        slab_a[QUAD, 2 * k : 2 * k + 2, :] = jnp.where(mine[0:2], x_v[8:10, pl.ds(start, TILE)], 0.0)

    pl.semaphore_wait(barrier, MEM - 1 + GX - 1 + GY - 1)

    cx = [remote(slab_a, got_x.at[k], xs.at[k], xr.at[k], x_peers[k]) for k in range(GX - 1)]
    for c in cx:
        c.start()
    feed(5)

    def pack(d, c):
        for q in range(CHUNKS):
            for u in range(QUADS):
                for t in range(QUAD):
                    col = pl.multiple_of(d * OWN + q * WIDTH + (u * QUAD + t) * TILE, TILE)
                    tails[d, q, 2 * t : 2 * t + 2, u * TILE : (u + 1) * TILE] = x_v[8:10, pl.ds(col, TILE)]
        return c

    lax.fori_loop(0, MEM, pack, 0)
    own = [
        pltpu.make_async_copy(x_hbm.at[0:8, columns(me, q)], recv1.at[me, q, :, 0:WIDTH], own_sem.at[q])
        for q in range(CHUNKS)
    ]
    for c in own:
        c.start()
    recv1[me, :, :, WIDTH:PACKED] = tails[me]
    feed(5)
    for c in cx:
        c.wait()
    slab_b[...] = slab_a[...] + got_x[0] + got_x[1] + got_x[2]
    cy = [remote(slab_b, got_y.at[k], ys.at[k], yr.at[k], y_peers[k]) for k in range(GY - 1)]
    for c in cy:
        c.start()
    feed(9)
    for c in cy:
        c.wait()
    slab_c[...] = slab_b[...] + got_y[0] + got_y[1] + got_y[2]
    cm = [remote(slab_c, got_m.at[me], ms.at[k], mr.at[k], mem_peers[k]) for k in range(MEM - 1)]
    for c in cm:
        c.start()
    got_m[me] = slab_c[...]
    feed(21)
    for c in cm:
        c.wait()

    for c in small[2:]:
        c.wait()
    slabs = gathered_quad(lambda s, t: got_m[s, t], lambda s: got_m[s, QUAD])
    sublane = lax.broadcasted_iota(jnp.int32, (TILE, OBS), 0)
    priors = []
    for k in range(BLOCKS):
        hot = jnp.where(sublane == off_ref[pl.ds(blocks[k], 1), :], 1.0, 0.0).astype(BF16)
        top, rest = split(slabs[k])
        low = (slabs[k] - top.astype(F32) - rest.astype(F32)).astype(BF16)
        priors.append(dot(top, hot) + (dot(rest, hot) + dot(low, hot)))
    pad = jnp.zeros((KDIM - 3 * M, OBS), BF16)
    none = jnp.zeros((M, KDIM), BF16)
    last = None
    for k in range(BLOCKS):
        b = blocks[k]
        val = val_ref[pl.ds(b, 1), :]
        err = err_ref[pl.ds(b, 1), :]
        ybar = jnp.sum(priors[k], axis=0, keepdims=True) * (1.0 / M)
        dev = priors[k] - ybar
        var = jnp.sum(dev * dev, axis=0, keepdims=True) * (1.0 / (M - 1.0))
        total = var + err
        lead = var / total * (val - ybar)
        shrink = jnp.sqrt(err / total) - 1.0
        dy = lead + shrink * dev
        weighted = dev * (1.0 / ((M - 1.0) * (var + 1e-05)))
        dh, dl = split(dy)
        wh, wl = split(weighted)
        wh = jnp.concatenate([wh, wh, wh, pad], axis=0)
        wl = jnp.concatenate([wl, wl, wl, pad], axis=0)
        tri = dot_nt(dh, wh) + (dot_nt(dh, wl) + dot_nt(dl, wh))
        left = left_form(tri)
        for j in range(k + 1, BLOCKS):
            on = mask_ref[b, tiles[j]].astype(F32)
            priors[j] = priors[j] + on * dot(left, stacked(priors[j]))
        at = 4 * (k // 2)
        if k % 2 == 0:
            hc[at] = none
            hc[at + 1] = left
            last = tri
        else:
            hc[at + 2] = left
            hc[at + 3] = left_form(last + tri + dot(left, stacked(last)))

    feed(len(pieces))
    for c in own:
        c.wait()
    for k in range(MEM - 1):
        out_tails(k).wait_recv()

    def out2(q, k):
        peer = mem_peers[k]
        return remote(send2.at[peer["mem"], q], recv2.at[me, q], ssem2.at[q, k], rsem2.at[q, k], peer)

    def keep(q):
        return pltpu.make_async_copy(send2.at[me, q], recv2.at[me, q], own_sem.at[q])

    first_tile = g * per + me * (OWN // TILE)

    def update(q, c):
        for k in range(MEM - 1):
            out1(q, k).wait_recv()
        for u in range(QUADS):
            quad = gathered_quad(
                lambda s, t: recv1[s, q, :, lanes(u * QUAD + t)], lambda s: recv1[s, q, :, lanes(QUADS * QUAD + u)]
            )
            pairs = [[], []]
            for t in range(QUAD):
                tile = first_tile + q * (QUADS * QUAD) + (u * QUAD + t)
                y = quad[t]
                for h in range(2):
                    on = [mask_ref[blocks[2 * h + k], tile] for k in range(2)]
                    y = y + dot(hc[4 * h + on[0] + 2 * on[1]], stacked(y))
                for d in range(MEM):
                    send2[d, q, :, lanes(u * QUAD + t)] = y[8 * d : 8 * d + 8]
                for h in range(2):
                    pairs[h].append(y[8 * MEM + 8 * h : 8 * MEM + 8 * h + 8])
            for h in range(2):
                back = pairs_transposed(pairs[h])
                for d in range(4):
                    send2[4 * h + d, q, :, lanes(QUADS * QUAD + u)] = back[d]
        for k in range(MEM - 1):
            out2(q, k).start()
        keep(q).start()
        return c

    lax.fori_loop(0, CHUNKS, update, 0)
    for q in range(CHUNKS):
        keep(q).wait()
        for k in range(MEM - 1):
            out2(q, k).wait()
    for piece in pieces[-DEPTH:]:
        piece.wait_send()


def unpack(packed, out, rows_v, main_sem, row_sem):
    started = []
    for d in range(MEM):
        for q in range(CHUNKS):
            cols = pl.ds(d * OWN + q * WIDTH, WIDTH)
            started.append(pltpu.make_async_copy(packed.at[d, q, :, 0:WIDTH], out.at[0:8, cols], main_sem.at[d, q]))
            started[-1].start()
    for d in range(MEM):
        for q in range(CHUNKS):
            for u in range(QUADS):
                for t in range(QUAD):
                    col = d * OWN + q * WIDTH + (u * QUAD + t) * TILE
                    rows_v[:, col : col + TILE] = packed[d, q, 2 * t : 2 * t + 2, WIDTH + u * TILE : WIDTH + (u + 1) * TILE]
        cols = pl.ds(d * OWN, OWN)
        started.append(pltpu.make_async_copy(rows_v.at[:, cols], out.at[8:10, cols], row_sem.at[d]))
        started[-1].start()
    for c in started:
        c.wait()


def on_device(state, obs_tile, obs_offset, obs_value, obs_error, loc_mask, block_order):
    whole = (MEM, CHUNKS, 8, PACKED)
    slab = (QUAD + 1, 8, TILE)
    hbm = pl.BlockSpec(memory_space=pltpu.HBM)
    dma = pltpu.SemaphoreType.DMA
    args = (state, obs_tile, block_order, obs_offset, obs_value, obs_error, loc_mask)
    args = [pltpu.with_memory_space_constraint(a, pltpu.HBM) for a in args]
    packed = pl.pallas_call(
        kernel,
        out_shape=jax.ShapeDtypeStruct(whole, F32),
        in_specs=[hbm] * 7,
        out_specs=hbm,
        scratch_shapes=[
            pltpu.VMEM((ROWS, LOCAL), F32),
            pltpu.SMEM((BLOCKS,), jnp.int32),
            pltpu.SMEM((BLOCKS,), jnp.int32),
            pltpu.VMEM((BLOCKS, OBS), jnp.int32),
            pltpu.VMEM((BLOCKS, OBS), F32),
            pltpu.VMEM((BLOCKS, OBS), F32),
            pltpu.SMEM((BLOCKS, GX * GY * LOCAL // TILE), jnp.int32),
            pltpu.VMEM((MEM, CHUNKS, 8, QUADS * TILE), F32),
            pltpu.VMEM(whole, F32),
            pltpu.VMEM(whole, F32),
            pltpu.VMEM(slab, F32),
            pltpu.VMEM(slab, F32),
            pltpu.VMEM(slab, F32),
            pltpu.VMEM((GX - 1,) + slab, F32),
            pltpu.VMEM((GY - 1,) + slab, F32),
            pltpu.VMEM((MEM,) + slab, F32),
            pltpu.VMEM((2 * BLOCKS, M, KDIM), BF16),
            dma((LOADS,)), dma((6,)), dma((CHUNKS,)),
            dma((CHUNKS, MEM - 1)), dma((CHUNKS, MEM - 1)),
            dma((MEM - 1,)), dma((MEM - 1,)),
            dma((CHUNKS, MEM - 1)), dma((CHUNKS, MEM - 1)),
            dma((GX - 1,)), dma((GX - 1,)),
            dma((GY - 1,)), dma((GY - 1,)),
            dma((MEM - 1,)), dma((MEM - 1,)),
        ],
        compiler_params=pltpu.CompilerParams(
            collective_id=0, has_side_effects=True, vmem_limit_bytes=40 << 20
        ),
        name="ensemble_update",
    )(*args)
    return pl.pallas_call(
        unpack,
        out_shape=jax.ShapeDtypeStruct(state.shape, F32),
        in_specs=[pl.BlockSpec(memory_space=pltpu.VMEM)],
        out_specs=hbm,
        scratch_shapes=[pltpu.VMEM((ROWS - 8, LOCAL), F32), dma((MEM, CHUNKS)), dma((MEM,))],
        compiler_params=pltpu.CompilerParams(vmem_limit_bytes=16 << 20),
        name="unpack",
    )(packed)


def solution(mesh):
    placed = (P("mem", "grid"), P(), P(), P(), P(), P(), P())
    return jax.shard_map(
        on_device, mesh=mesh, in_specs=placed, out_specs=P("mem", "grid"), check_vma=False
    )
```

```python
import jax
import jax.numpy as jnp
from jax import lax
from jax.experimental import pallas as pl
from jax.experimental.pallas import tpu as pltpu
from jax.sharding import PartitionSpec as P

MESH = pl.DeviceIdType.MESH
F32, BF16 = jnp.float32, jnp.bfloat16

MEM = 8
GX, GY = 4, 4
ROWS = 10
M = MEM * ROWS
OBS = 256
BLOCKS = 4
TILE = 128
QUAD = 4
CHUNKS = 2
QUADS = 4
WIDTH = QUADS * QUAD * TILE
OWN = CHUNKS * WIDTH
LOCAL = MEM * OWN
PACKED = WIDTH + QUADS * TILE
DEPTH = 21
LOADS = 4
HOPS = [(1, 0), (3, 0), (2, 1), (1, 1), (3, 1), (2, 0), (0, 1)]
KDIM = 256


def split(x):
    hi = x.astype(BF16)
    lo = (x - hi.astype(F32)).astype(BF16)
    return hi, lo


def stacked(x):
    hi, lo = split(x)
    return jnp.concatenate([hi, lo, hi, jnp.zeros((KDIM - 3 * M, x.shape[1]), BF16)], axis=0)


def left_form(tri):
    hi, lo = split(tri)
    lane = lax.broadcasted_iota(jnp.int32, tri.shape, 1)
    return jnp.where(lane < 2 * M, hi.astype(F32), lo.astype(F32)).astype(BF16)


def dot(a, b):
    return jnp.dot(a, b, preferred_element_type=F32)


def dot_nt(a, b):
    return lax.dot_general(a, b, (((1,), (1,)), ((), ())), preferred_element_type=F32)


def pairs_transposed(regs):
    pair = lax.broadcasted_iota(jnp.int32, (8, TILE), 0) // 2
    out = []
    for j in range(QUAD):
        acc = None
        for i in range(QUAD):
            moved = regs[i] if i == j else pltpu.roll(regs[i], (2 * (i - j)) % 8, 0)
            acc = moved if acc is None else jnp.where(pair == i, moved, acc)
        out.append(acc)
    return out


def gathered_quad(main, tail):
    tails = [pairs_transposed([tail(4 * h + s) for s in range(4)]) for h in range(2)]
    tiles = []
    for t in range(QUAD):
        tiles.append(jnp.concatenate([main(s, t) for s in range(MEM)] + [tails[0][t], tails[1][t]], axis=0))
    return tiles


def lanes(tile):
    return pl.ds(tile * TILE, TILE)


def kernel(
    x_hbm, tile_hbm, order_hbm, off_hbm, val_hbm, err_hbm, mask_hbm,
    recv2,
    x_v, tile_ref, order_ref, off_ref, val_ref, err_ref, mask_ref,
    tails, recv1, send2, slab_a, slab_b, slab_c, got_x, got_y, got_m, hc,
    x_sem, in_sem, own_sem, ssem1, rsem1, tsend, trecv, ssem2, rsem2, xs, xr, ys, yr, ms, mr,
):
    me = lax.axis_index("mem")
    g = lax.axis_index("grid")
    gx, gy = g // GY, lax.rem(g, GY)

    def remote(src, dst, s, r, peer):
        return pltpu.make_async_remote_copy(
            src_ref=src, dst_ref=dst, send_sem=s, recv_sem=r, device_id=peer, device_id_type=MESH
        )

    z, core = me // 2, lax.rem(me, 2)
    mem_peers = [{"mem": lax.rem(z + dz, MEM // 2) * 2 + lax.rem(core + dc, 2)} for dz, dc in HOPS]
    x_peers = [{"grid": lax.rem(gx + k, GX) * GY + gy} for k in range(1, GX)]
    y_peers = [{"grid": gx * GY + lax.rem(gy + k, GY)} for k in range(1, GY)]
    barrier = pltpu.get_barrier_semaphore()
    for peer in mem_peers + x_peers + y_peers:
        pl.semaphore_signal(barrier, inc=1, device_id=peer, device_id_type=MESH)

    small = [
        pltpu.make_async_copy(src, dst, in_sem.at[i])
        for i, (src, dst) in enumerate([
            (order_hbm, order_ref), (tile_hbm, tile_ref), (mask_hbm, mask_ref),
            (off_hbm, off_ref), (val_hbm, val_ref), (err_hbm, err_ref),
        ])
    ]
    load_x = []
    for i in range(LOADS):
        cols = pl.ds(i * (LOCAL // LOADS), LOCAL // LOADS)
        load_x.append(pltpu.make_async_copy(x_hbm.at[:, cols], x_v.at[:, cols], x_sem.at[i]))
    for c in small[:2] + load_x + small[2:]:
        c.start()

    def columns(d, q):
        return pl.ds(pl.multiple_of(d * OWN + q * WIDTH, WIDTH), WIDTH)

    def out1(q, k):
        peer = mem_peers[k]
        src = x_hbm.at[0:8, columns(peer["mem"], q)]
        return remote(src, recv1.at[me, q, :, 0:WIDTH], ssem1.at[q, k], rsem1.at[q, k], peer)

    def out_tails(k):
        peer = mem_peers[k]
        dst = recv1.at[me, :, :, WIDTH:PACKED]
        return remote(tails.at[peer["mem"]], dst, tsend.at[k], trecv.at[k], peer)

    pieces = [out1(q, k) for q in range(CHUNKS) for k in range(MEM - 1)]
    pieces[7:7] = [out_tails(k) for k in range(MEM - 1)]

    def feed(upto):
        while fed[0] < upto:
            if fed[0] >= DEPTH:
                pieces[fed[0] - DEPTH].wait_send()
            pieces[fed[0]].start()
            fed[0] += 1

    fed = [0]
    pl.semaphore_wait(barrier, MEM - 1 + GX - 1 + GY - 1)

    feed(3)
    for c in small[:2] + load_x:
        c.wait()

    blocks = [order_ref[k] for k in range(BLOCKS)]
    tiles = [tile_ref[blocks[k]] for k in range(BLOCKS)]
    per = LOCAL // TILE
    for k in range(BLOCKS):
        within = lax.rem(tiles[k], per)
        start = within * TILE
        away = tiles[k] - within - g * per
        mine = jnp.full((8, TILE), away, jnp.int32) == 0
        slab_a[k] = jnp.where(mine, x_v[0:8, pl.ds(start, TILE)], 0.0)
        slab_a[QUAD, 2 * k : 2 * k + 2, :] = jnp.where(mine[0:2], x_v[8:10, pl.ds(start, TILE)], 0.0)

    cx = [remote(slab_a, got_x.at[k], xs.at[k], xr.at[k], x_peers[k]) for k in range(GX - 1)]
    for c in cx:
        c.start()
    feed(5)

    def pack(d, c):
        for q in range(CHUNKS):
            for u in range(QUADS):
                for t in range(QUAD):
                    col = pl.multiple_of(d * OWN + q * WIDTH + (u * QUAD + t) * TILE, TILE)
                    tails[d, q, 2 * t : 2 * t + 2, u * TILE : (u + 1) * TILE] = x_v[8:10, pl.ds(col, TILE)]
        return c

    lax.fori_loop(0, MEM, pack, 0)
    own = [
        pltpu.make_async_copy(x_hbm.at[0:8, columns(me, q)], recv1.at[me, q, :, 0:WIDTH], own_sem.at[q])
        for q in range(CHUNKS)
    ]
    for c in own:
        c.start()
    recv1[me, :, :, WIDTH:PACKED] = tails[me]
    feed(5)
    for c in cx:
        c.wait()
    slab_b[...] = slab_a[...] + got_x[0] + got_x[1] + got_x[2]
    cy = [remote(slab_b, got_y.at[k], ys.at[k], yr.at[k], y_peers[k]) for k in range(GY - 1)]
    for c in cy:
        c.start()
    feed(9)
    for c in cy:
        c.wait()
    slab_c[...] = slab_b[...] + got_y[0] + got_y[1] + got_y[2]
    cm = [remote(slab_c, got_m.at[me], ms.at[k], mr.at[k], mem_peers[k]) for k in range(MEM - 1)]
    for c in cm:
        c.start()
    got_m[me] = slab_c[...]
    feed(21)
    for c in cm:
        c.wait()

    for c in small[2:]:
        c.wait()
    slabs = gathered_quad(lambda s, t: got_m[s, t], lambda s: got_m[s, QUAD])
    sublane = lax.broadcasted_iota(jnp.int32, (TILE, OBS), 0)
    priors = []
    for k in range(BLOCKS):
        hot = jnp.where(sublane == off_ref[pl.ds(blocks[k], 1), :], 1.0, 0.0).astype(BF16)
        top, rest = split(slabs[k])
        low = (slabs[k] - top.astype(F32) - rest.astype(F32)).astype(BF16)
        priors.append(dot(top, hot) + (dot(rest, hot) + dot(low, hot)))
    pad = jnp.zeros((KDIM - 3 * M, OBS), BF16)
    none = jnp.zeros((M, KDIM), BF16)
    last = None
    for k in range(BLOCKS):
        b = blocks[k]
        val = val_ref[pl.ds(b, 1), :]
        err = err_ref[pl.ds(b, 1), :]
        ybar = jnp.sum(priors[k], axis=0, keepdims=True) * (1.0 / M)
        dev = priors[k] - ybar
        var = jnp.sum(dev * dev, axis=0, keepdims=True) * (1.0 / (M - 1.0))
        total = var + err
        lead = var / total * (val - ybar)
        shrink = jnp.sqrt(err / total) - 1.0
        dy = lead + shrink * dev
        weighted = dev * (1.0 / ((M - 1.0) * (var + 1e-05)))
        dh, dl = split(dy)
        wh, wl = split(weighted)
        wh = jnp.concatenate([wh, wh, wh, pad], axis=0)
        wl = jnp.concatenate([wl, wl, wl, pad], axis=0)
        tri = dot_nt(dh, wh) + (dot_nt(dh, wl) + dot_nt(dl, wh))
        left = left_form(tri)
        for j in range(k + 1, BLOCKS):
            on = mask_ref[b, tiles[j]].astype(F32)
            priors[j] = priors[j] + on * dot(left, stacked(priors[j]))
        at = 4 * (k // 2)
        if k % 2 == 0:
            hc[at] = none
            hc[at + 1] = left
            last = tri
        else:
            hc[at + 2] = left
            hc[at + 3] = left_form(last + tri + dot(left, stacked(last)))

    feed(len(pieces))
    for c in own:
        c.wait()
    for k in range(MEM - 1):
        out_tails(k).wait_recv()

    def out2(q, k):
        peer = mem_peers[k]
        return remote(send2.at[peer["mem"], q], recv2.at[me, q], ssem2.at[q, k], rsem2.at[q, k], peer)

    def keep(q):
        return pltpu.make_async_copy(send2.at[me, q], recv2.at[me, q], own_sem.at[q])

    first_tile = g * per + me * (OWN // TILE)

    def update(q, c):
        for k in range(MEM - 1):
            out1(q, k).wait_recv()
        for u in range(QUADS):
            quad = gathered_quad(
                lambda s, t: recv1[s, q, :, lanes(u * QUAD + t)], lambda s: recv1[s, q, :, lanes(QUADS * QUAD + u)]
            )
            pairs = [[], []]
            for t in range(QUAD):
                tile = first_tile + q * (QUADS * QUAD) + (u * QUAD + t)
                y = quad[t]
                for h in range(2):
                    on = [mask_ref[blocks[2 * h + k], tile] for k in range(2)]
                    y = y + dot(hc[4 * h + on[0] + 2 * on[1]], stacked(y))
                for d in range(MEM):
                    send2[d, q, :, lanes(u * QUAD + t)] = y[8 * d : 8 * d + 8]
                for h in range(2):
                    pairs[h].append(y[8 * MEM + 8 * h : 8 * MEM + 8 * h + 8])
            for h in range(2):
                back = pairs_transposed(pairs[h])
                for d in range(4):
                    send2[4 * h + d, q, :, lanes(QUADS * QUAD + u)] = back[d]
        for k in range(MEM - 1):
            out2(q, k).start()
        keep(q).start()
        return c

    lax.fori_loop(0, CHUNKS, update, 0)
    for q in range(CHUNKS):
        keep(q).wait()
        for k in range(MEM - 1):
            out2(q, k).wait()
    for piece in pieces[-DEPTH:]:
        piece.wait_send()


def unpack(packed, out, rows_v, main_sem, row_sem):
    started = []
    for d in range(MEM):
        for q in range(CHUNKS):
            cols = pl.ds(d * OWN + q * WIDTH, WIDTH)
            started.append(pltpu.make_async_copy(packed.at[d, q, :, 0:WIDTH], out.at[0:8, cols], main_sem.at[d, q]))
            started[-1].start()
    for d in range(MEM):
        for q in range(CHUNKS):
            for u in range(QUADS):
                for t in range(QUAD):
                    col = d * OWN + q * WIDTH + (u * QUAD + t) * TILE
                    rows_v[:, col : col + TILE] = packed[d, q, 2 * t : 2 * t + 2, WIDTH + u * TILE : WIDTH + (u + 1) * TILE]
        cols = pl.ds(d * OWN, OWN)
        started.append(pltpu.make_async_copy(rows_v.at[:, cols], out.at[8:10, cols], row_sem.at[d]))
        started[-1].start()
    for c in started:
        c.wait()


def on_device(state, obs_tile, obs_offset, obs_value, obs_error, loc_mask, block_order):
    whole = (MEM, CHUNKS, 8, PACKED)
    slab = (QUAD + 1, 8, TILE)
    hbm = pl.BlockSpec(memory_space=pltpu.HBM)
    dma = pltpu.SemaphoreType.DMA
    args = (state, obs_tile, block_order, obs_offset, obs_value, obs_error, loc_mask)
    args = [pltpu.with_memory_space_constraint(a, pltpu.HBM) for a in args]
    packed = pl.pallas_call(
        kernel,
        out_shape=jax.ShapeDtypeStruct(whole, F32),
        in_specs=[hbm] * 7,
        out_specs=hbm,
        scratch_shapes=[
            pltpu.VMEM((ROWS, LOCAL), F32),
            pltpu.SMEM((BLOCKS,), jnp.int32),
            pltpu.SMEM((BLOCKS,), jnp.int32),
            pltpu.VMEM((BLOCKS, OBS), jnp.int32),
            pltpu.VMEM((BLOCKS, OBS), F32),
            pltpu.VMEM((BLOCKS, OBS), F32),
            pltpu.SMEM((BLOCKS, GX * GY * LOCAL // TILE), jnp.int32),
            pltpu.VMEM((MEM, CHUNKS, 8, QUADS * TILE), F32),
            pltpu.VMEM(whole, F32),
            pltpu.VMEM(whole, F32),
            pltpu.VMEM(slab, F32),
            pltpu.VMEM(slab, F32),
            pltpu.VMEM(slab, F32),
            pltpu.VMEM((GX - 1,) + slab, F32),
            pltpu.VMEM((GY - 1,) + slab, F32),
            pltpu.VMEM((MEM,) + slab, F32),
            pltpu.VMEM((2 * BLOCKS, M, KDIM), BF16),
            dma((LOADS,)), dma((6,)), dma((CHUNKS,)),
            dma((CHUNKS, MEM - 1)), dma((CHUNKS, MEM - 1)),
            dma((MEM - 1,)), dma((MEM - 1,)),
            dma((CHUNKS, MEM - 1)), dma((CHUNKS, MEM - 1)),
            dma((GX - 1,)), dma((GX - 1,)),
            dma((GY - 1,)), dma((GY - 1,)),
            dma((MEM - 1,)), dma((MEM - 1,)),
        ],
        compiler_params=pltpu.CompilerParams(
            collective_id=0, has_side_effects=True, vmem_limit_bytes=40 << 20
        ),
        name="ensemble_update",
    )(*args)
    return pl.pallas_call(
        unpack,
        out_shape=jax.ShapeDtypeStruct(state.shape, F32),
        in_specs=[pl.BlockSpec(memory_space=pltpu.VMEM)],
        out_specs=hbm,
        scratch_shapes=[pltpu.VMEM((ROWS - 8, LOCAL), F32), dma((MEM, CHUNKS)), dma((MEM,))],
        compiler_params=pltpu.CompilerParams(vmem_limit_bytes=16 << 20),
        name="unpack",
    )(packed)


def solution(mesh):
    placed = (P("mem", "grid"), P(), P(), P(), P(), P(), P())
    return jax.shard_map(
        on_device, mesh=mesh, in_specs=placed, out_specs=P("mem", "grid"), check_vma=False
    )
```
